32 devices in a mesh: cuts: 4 (over y, x), det: 2 (over core), bank: 4 (over z).
Axes of the slice: x: 2, y: 2, z: 4, core: 2. Of those that a mesh axis runs over, the one named last changes fastest.
Arguments:
- strain: bfloat16 [4, 2, 6144], P('cuts', 'det'), may hold values from -6 to 6
- filters: bfloat16 [16, 256, 2048], P(('bank', 'cuts')), parts along dimension 0, may hold values from -0.125 to 0.125
- recon_weights: bfloat16 [16, 128, 256], P(('bank', 'cuts')), parts along dimension 0, may hold values from -0.1875 to 0.1875
- row_spans: int32 [512], P('bank'), parts along dimension 0, may hold values from 1 to 4
- slice_rates: int32 [4], replicated, may hold values from 1 to 8, as said below
- delays: int32 [64, 2], replicated, may hold values from 0 to 47
- antenna: float32 [64, 2], replicated, may hold values from 0.2 to 1
Outputs:
- peak_amplitude: float32 [512, 4096], P(('bank', 'cuts', 'det')), parts along dimension 0
The draws below stay inside these ranges and needn't reach their ends.
There are 4 independent parts, one for each index of `bank`. The reference program is written for one: setup_inputs(seed, part) draws one part's arguments, and reference() takes and returns one part's arrays. A program takes and returns all parts, laid end to end along the dimension named above; an argument that names none is the same for every part. Nothing has to cross between parts.
Inputs may be any that keep to these rules, and one draw needn't show every extreme that they name: `slice_rates`: every entry is a power of two; entries never fall along the slices; the first is 1 and the last is 8.
All inputs are finite; a program needn't handle non-finite values.
Results may differ from the reference program's by a relative error of at most 0.0014.
Values sent between devices are 32-bit elements; how exact they have to be, the bound alone decides.
A program may use at most 64 MiB of HBM per device.

```python
import jax
import jax.numpy as jnp
from jax import lax

WIN = 4096
TAPS = 2048
BASES = 256
FMAX = 8
DIRS = 64
MAXD = 48
SLICES = 4
DETS = 2
ROWS = 128
N_CUTS = 4


def draw_slice_rates(key, part):
    top_level = FMAX.bit_length() - 1
    levels = jnp.sort(jax.random.randint(key, (SLICES,), 0, top_level + 1))
    levels = levels.at[0].set(0).at[SLICES - 1].set(top_level)
    return jnp.left_shift(jnp.ones((SLICES,), jnp.int32), levels).astype(jnp.int32)


def place_ends(values, stream_key, least, high):
    extent = values.shape
    index_at = [jax.random.randint(jax.random.fold_in(stream_key, axis), (), 0, extent[axis]) for axis in range(len(extent))]
    values = values.at[tuple(index_at)].set(least)
    longest = extent.index(max(extent))
    index_at[longest] = (index_at[longest] + 1) % extent[longest]
    return values.at[tuple(index_at)].set(high)


def level_of(key, shape, shards, smallest, largest):
    def one(dim, parts):
        steps = jax.random.uniform(jax.random.fold_in(jax.random.fold_in(key, 6), dim), (parts,), jnp.float32, smallest / len(shards), largest / len(shards))
        return jnp.repeat(jnp.exp(steps), shape[dim] // parts).reshape((-1,) + (1,) * (len(shape) - dim - 1))

    gain = one(*shards[0])
    for cut in shards[1:]:
        gain = gain * one(*cut)
    return gain


def noise(rng, dims, deviation, most, cuts=(), kind=jnp.bfloat16):
    level = level_of(rng, dims, cuts, -0.22, 0.18) if cuts else 1.0
    drawn = jax.random.normal(rng, dims, jnp.float32) * deviation * level
    return jnp.minimum(jnp.maximum(drawn, -most), most).astype(kind)


def setup_inputs(seed: int = 0, part: int = 0) -> dict:
    key_of = jax.random.split(jax.random.key(seed), 8)
    own_keys = jax.random.split(jax.random.fold_in(key_of[7], part), 8)
    return {
        "strain": noise(key_of[0], (SLICES, DETS, TAPS + WIN), 1.0, 6.0, ((0, 4), (1, 2))),
        "filters": noise(own_keys[1], (SLICES, BASES, TAPS), TAPS ** -0.5, 0.125, ((0, 4),)),
        "recon_weights": noise(own_keys[2], (SLICES, ROWS, BASES), (BASES * N_CUTS) ** -0.5, 0.1875, ((0, 4),)),
        "row_spans": place_ends(jax.random.randint(own_keys[3], (ROWS,), 1, SLICES + 1), jax.random.fold_in(own_keys[3], 1), 1, SLICES).astype(jnp.int32),
        "slice_rates": draw_slice_rates(jax.random.fold_in(key_of[7], 71), part),
        "delays": place_ends(jax.random.randint(key_of[5], (DIRS, DETS), 0, MAXD), jax.random.fold_in(key_of[5], 1), 0, MAXD - 1).astype(jnp.int32),
        "antenna": jnp.clip(jax.random.uniform(key_of[6], (DIRS, DETS), jnp.float32, 0.2, 1.0), 0.2, 1.0),
    }


def filter_reference(samples, bank):
    size = 2 * TAPS + WIN
    spectrum = jnp.fft.rfft(samples.astype(jnp.float32), n=size)
    kernel = jnp.fft.rfft(bank.astype(jnp.float32), n=size, axis=1)
    convolved = jnp.fft.irfft(kernel * spectrum[None, :], n=size, axis=1)
    return convolved[:, TAPS:TAPS + WIN].astype(jnp.bfloat16)


def coherent(series, delays, antenna):
    detectors, height, window = series.shape
    padded = jnp.concatenate([series, jnp.zeros((detectors, height, MAXD), series.dtype)], axis=2)

    def direction(number, highest):
        summed = jnp.zeros((height, window), jnp.float32)
        for detector in range(detectors):
            shifted = lax.dynamic_slice_in_dim(padded[detector], delays[number, detector], window, 1)
            summed = summed + antenna[number, detector] * shifted
        return jnp.maximum(highest, jnp.abs(summed))

    return lax.fori_loop(0, delays.shape[0], direction, jnp.zeros((height, window), jnp.float32))


def reference(strain, filters, recon_weights, row_spans, slice_rates, delays, antenna):
    moments = jnp.arange(WIN, dtype=jnp.int32)

    def one_slice(total, inputs):
        samples, bank, weights, factor, number = inputs
        filtered = jax.vmap(filter_reference, in_axes=(0, None))(samples, bank)
        rebuilt = jnp.einsum("rb,kbw->krw", weights.astype(jnp.float32), filtered.astype(jnp.float32))
        keeping = (number < row_spans).astype(jnp.float32)
        terms = rebuilt * keeping[None, :, None]
        widened = jnp.take(terms, moments // factor, axis=2)
        return total + widened, None

    numbers = jnp.arange(SLICES, dtype=jnp.int32)
    combined, unused = lax.scan(one_slice, jnp.zeros((DETS, ROWS, WIN), jnp.float32), (strain, filters, recon_weights, slice_rates, numbers))
    return coherent(combined, delays, antenna)
```

```python
import functools

import jax
import jax.numpy as jnp
from jax import lax
from jax.experimental import pallas as pl
from jax.experimental.pallas import tpu as pltpu
from jax.sharding import PartitionSpec as P

MESH = pl.DeviceIdType.MESH
LANES = 128
WIDE = 256


def exchange_kernel(
    cuts, dets, spans_ref, strain_ref, filters_ref, weights_ref, bank_ref, series_ref,
    bank_stage, series_stage, bank_send, bank_recv, series_send, series_recv, keep_sem,
):
    me = lax.axis_index("cuts")
    core = lax.axis_index("det")
    peers = []
    for step in range(cuts):
        for turn in range(dets):
            if step or turn:
                peers.append((step, turn))
    barrier = pltpu.get_barrier_semaphore()
    for step, turn in peers:
        where = {"cuts": lax.rem(me + step, cuts), "det": lax.rem(core + turn, dets)}
        pl.semaphore_signal(barrier, inc=1, device_id=where, device_id_type=MESH)

    series_stage[...] = strain_ref[...].astype(jnp.float32)
    rows = weights_ref.shape[0]
    share = rows // cuts // dets
    live = (me < spans_ref[...]).astype(jnp.float32)
    across = lax.broadcasted_iota(jnp.int32, (rows, rows), 1)
    down = lax.broadcasted_iota(jnp.int32, (rows, rows), 0)
    keep = jnp.sum(jnp.where(across == down, live, 0.0), axis=1, keepdims=True)
    kept = (weights_ref[...].astype(jnp.float32) * keep).astype(jnp.bfloat16)
    parts = []
    for cut in range(cuts):
        low = kept[(cut * dets) * share : (cut * dets + 1) * share]
        for det in range(1, dets):
            other = kept[(cut * dets + det) * share : (cut * dets + det + 1) * share]
            low = jnp.where(core == det, other, low)
        parts.append(low)
    stacked = jnp.concatenate(parts, axis=0)
    taps = filters_ref.shape[1]
    for first in range(0, taps, WIDE):
        block = jnp.dot(stacked, filters_ref[:, first : first + WIDE], preferred_element_type=jnp.float32)
        for cut in range(cuts):
            bank_stage[cut, :, first : first + WIDE] = block[cut * share : (cut + 1) * share]

    pl.semaphore_wait(barrier, len(peers))
    mine = me * dets + core
    copies = []
    for number, (step, turn) in enumerate(peers):
        where = {"cuts": lax.rem(me + step, cuts), "det": lax.rem(core + turn, dets)}
        copies.append(pltpu.make_async_remote_copy(
            src_ref=series_stage, dst_ref=series_ref.at[mine],
            send_sem=series_send.at[number], recv_sem=series_recv.at[number],
            device_id=where, device_id_type=MESH,
        ))
    for step in range(1, cuts):
        target = lax.rem(me + step, cuts)
        copies.append(pltpu.make_async_remote_copy(
            src_ref=bank_stage.at[target], dst_ref=bank_ref.at[me],
            send_sem=bank_send.at[step - 1], recv_sem=bank_recv.at[step - 1],
            device_id={"cuts": target}, device_id_type=MESH,
        ))
    for copy in copies:
        copy.start()
    own = [
        pltpu.make_async_copy(series_stage, series_ref.at[mine], keep_sem.at[0]),
        pltpu.make_async_copy(bank_stage.at[me], bank_ref.at[me], keep_sem.at[1]),
    ]
    for copy in own:
        copy.start()
    for copy in own:
        copy.wait()
    for copy in copies:
        copy.wait()


def exchange(spans, strain, filters, weights, cuts, dets):
    rows = weights.shape[0] // cuts // dets
    taps = filters.shape[1]
    length = strain.shape[-1]
    vmem = pl.BlockSpec(memory_space=pltpu.VMEM)
    return pl.pallas_call(
        functools.partial(exchange_kernel, cuts, dets),
        out_shape=(
            jax.ShapeDtypeStruct((cuts, rows, taps), jnp.float32),
            jax.ShapeDtypeStruct((cuts * dets, 1, length), jnp.float32),
        ),
        in_specs=[vmem] * 4,
        out_specs=(vmem, vmem),
        scratch_shapes=[
            pltpu.VMEM((cuts, rows, taps), jnp.float32),
            pltpu.VMEM((1, length), jnp.float32),
            pltpu.SemaphoreType.DMA((cuts - 1,)),
            pltpu.SemaphoreType.DMA((cuts - 1,)),
            pltpu.SemaphoreType.DMA((cuts * dets - 1,)),
            pltpu.SemaphoreType.DMA((cuts * dets - 1,)),
            pltpu.SemaphoreType.DMA((2,)),
        ],
        compiler_params=pltpu.CompilerParams(collective_id=0, has_side_effects=True),
    )(spans, strain, filters, weights)


def search_kernel(
    rates_ref, delays_ref, antenna_ref, bank_ref, series_ref, peak_ref,
    toeplitz, total, combined, turned,
):
    slices, rows, taps = bank_ref.shape
    dets = series_ref.shape[0] // slices
    window = peak_ref.shape[1]
    tiles = window // LANES
    pieces = taps // WIDE
    combined[...] = jnp.zeros(combined.shape, jnp.float32)
    lane = lax.broadcasted_iota(jnp.int32, (rows, LANES), 1)

    def one_slice(number, carry):
        rate = rates_ref[number]
        level = (rate > 1).astype(jnp.int32) + (rate > 3).astype(jnp.int32) + (rate > 7).astype(jnp.int32)
        blocks = lax.shift_right_logical(jnp.int32(window // WIDE), level)
        taps_all = bank_ref[number].astype(jnp.bfloat16)
        stacked = jnp.concatenate(
            [taps_all[:, piece * WIDE : (piece + 1) * WIDE] for piece in range(pieces)], axis=0
        )

        total[...] = jnp.zeros(total.shape, jnp.float32)

        def build(step, c):
            for det in range(dets):
                for odd in range(2):
                    at = 2 * step + odd
                    piece = series_ref[number * dets + det, :, pl.ds(pl.multiple_of(at * LANES, LANES), 2 * LANES)]
                    spread = jnp.broadcast_to(piece, (LANES, 2 * LANES))
                    rolled = pltpu.roll(spread, 0, 1, stride=1, stride_axis=0)
                    toeplitz[det, at] = rolled[:, LANES:].astype(jnp.bfloat16)
            return c

        steps = blocks + pieces - 1
        lax.fori_loop(0, steps, build, 0)
        for det in range(dets):
            at = 2 * steps
            piece = series_ref[number * dets + det, :, pl.ds(pl.multiple_of(at * LANES, LANES), 2 * LANES)]
            spread = jnp.broadcast_to(piece, (LANES, 2 * LANES))
            rolled = pltpu.roll(spread, 0, 1, stride=1, stride_axis=0)
            toeplitz[det, at] = rolled[:, LANES:].astype(jnp.bfloat16)

        def convolve(step, c):
            for det in range(dets):
                low = toeplitz[det, 2 * step]
                middle = toeplitz[det, 2 * step + 1]
                high = toeplitz[det, 2 * step + 2]
                square = jnp.concatenate(
                    [jnp.concatenate([middle, high], axis=1), jnp.concatenate([low, middle], axis=1)], axis=0
                )
                result = jnp.dot(stacked, square, preferred_element_type=jnp.float32)
                for piece in range(pieces):
                    for half in range(2):
                        at = 2 * (step + piece) + half
                        total[det, at] += result[
                            piece * rows : (piece + 1) * rows, half * LANES : (half + 1) * LANES
                        ]
            return c

        lax.fori_loop(0, steps, convolve, 0)

        skip = 2 * (pieces - 1)
        inner = lax.shift_right_logical(lane, level)
        for tile in range(tiles):
            source = lax.shift_right_logical(jnp.int32(tile), level)
            part = tile - lax.shift_left(source, level)
            index = inner + part * lax.shift_right_logical(jnp.int32(LANES), level)
            for det in range(dets):
                values = total[det, skip + source]
                combined[det, tile] += jnp.take_along_axis(values, index, axis=1)
        return carry

    lax.fori_loop(0, slices, one_slice, 0)

    groups = LANES // rows
    apart = tiles // groups
    for det in range(dets):
        for offset in range(apart + 1):
            block = jnp.concatenate(
                [combined[det, group * apart + offset] for group in range(groups)], axis=0
            )
            turned[det, offset * LANES : (offset + 1) * LANES] = block.T

    for offset in range(apart):
        def direction(number, highest):
            summed = None
            for det in range(dets):
                start = delays_ref[number, det] + offset * LANES
                term = antenna_ref[number, det] * turned[det, pl.ds(start, LANES), :]
                summed = term if summed is None else summed + term
            return jnp.maximum(highest, jnp.abs(summed))

        highest = lax.fori_loop(
            0, delays_ref.shape[0], direction, jnp.zeros((LANES, LANES), jnp.float32), unroll=2
        )
        back = highest.T
        for group in range(groups):
            at = (group * apart + offset) * LANES
            peak_ref[:, at : at + LANES] = back[group * rows : (group + 1) * rows]


def search(rates, delays, antenna, bank, series):
    slices, rows, taps = bank.shape
    dets = series.shape[0] // slices
    window = series.shape[2] - taps
    tiles = window // LANES
    pieces = taps // WIDE
    groups = LANES // rows
    apart = tiles // groups
    smem = pl.BlockSpec(memory_space=pltpu.SMEM)
    vmem = pl.BlockSpec(memory_space=pltpu.VMEM)
    return pl.pallas_call(
        search_kernel,
        out_shape=jax.ShapeDtypeStruct((rows, window), jnp.float32),
        in_specs=[smem, smem, smem, vmem, vmem],
        out_specs=vmem,
        scratch_shapes=[
            pltpu.VMEM((dets, series.shape[2] // LANES, LANES, LANES), jnp.bfloat16),
            pltpu.VMEM((dets, tiles + 4 * pieces, rows, LANES), jnp.float32),
            pltpu.VMEM((dets, tiles + apart, rows, LANES), jnp.float32),
            pltpu.VMEM((dets, (apart + 1) * LANES, LANES), jnp.float32),
        ],
    )(rates, delays, antenna, bank, series)


def shards(strain, filters, recon_weights, row_spans, slice_rates, delays, antenna):
    cuts = lax.axis_size("cuts")
    dets = lax.axis_size("det")
    bank, series = exchange(
        row_spans.reshape(1, -1), strain.reshape(1, -1), filters[0], recon_weights[0], cuts, dets
    )
    return search(slice_rates, delays, antenna, bank, series)


def solution(mesh):
    placed = (
        P("cuts", "det", None),
        P(("bank", "cuts"), None, None),
        P(("bank", "cuts"), None, None),
        P("bank"),
        P(),
        P(),
        P(),
    )
    return jax.shard_map(
        shards,
        mesh=mesh,
        in_specs=placed,
        out_specs=P(("bank", "cuts", "det"), None),
        check_vma=False,
    )
```

```python
import functools

import jax
import jax.numpy as jnp
from jax import lax
from jax.experimental import pallas as pl
from jax.experimental.pallas import tpu as pltpu
from jax.sharding import PartitionSpec as P

MESH = pl.DeviceIdType.MESH
LANES = 128
WIDE = 256
BATCH = 4
CHUNK = 64


def exchange_kernel(
    cuts, dets, spans_ref, strain_ref, filters_ref, weights_ref, bank_ref, series_ref,
    bank_stage, series_stage, bank_send, bank_recv, series_send, series_recv, keep_sem,
):
    me = lax.axis_index("cuts")
    core = lax.axis_index("det")
    peers = []
    for step in range(cuts):
        for turn in range(dets):
            if step or turn:
                peers.append((step, turn))
    barrier = pltpu.get_barrier_semaphore()
    for step, turn in peers:
        where = {"cuts": lax.rem(me + step, cuts), "det": lax.rem(core + turn, dets)}
        pl.semaphore_signal(barrier, inc=1, device_id=where, device_id_type=MESH)

    length = strain_ref.shape[1]
    series_stage[...] = strain_ref[...].astype(jnp.float32)
    for row in range(cuts * dets):
        series_ref[row, :, length:] = jnp.zeros((1, series_ref.shape[2] - length), jnp.float32)
    rows = weights_ref.shape[0]
    share = rows // cuts // dets
    live = (me < spans_ref[...]).astype(jnp.float32)
    across = lax.broadcasted_iota(jnp.int32, (rows, rows), 1)
    down = lax.broadcasted_iota(jnp.int32, (rows, rows), 0)
    keep = jnp.sum(jnp.where(across == down, live, 0.0), axis=1, keepdims=True)
    kept = (weights_ref[...].astype(jnp.float32) * keep).astype(jnp.bfloat16)
    parts = []
    for cut in range(cuts):
        low = kept[(cut * dets) * share : (cut * dets + 1) * share]
        for det in range(1, dets):
            other = kept[(cut * dets + det) * share : (cut * dets + det + 1) * share]
            low = jnp.where(core == det, other, low)
        parts.append(low)
    stacked = jnp.concatenate(parts, axis=0)
    taps = filters_ref.shape[1]
    for first in range(0, taps, WIDE):
        block = jnp.dot(stacked, filters_ref[:, first : first + WIDE], preferred_element_type=jnp.float32)
        for cut in range(cuts):
            bank_stage[cut, :, first : first + WIDE] = block[cut * share : (cut + 1) * share]

    pl.semaphore_wait(barrier, len(peers))
    mine = me * dets + core
    copies = []
    for number, (step, turn) in enumerate(peers):
        where = {"cuts": lax.rem(me + step, cuts), "det": lax.rem(core + turn, dets)}
        copies.append(pltpu.make_async_remote_copy(
            src_ref=series_stage, dst_ref=series_ref.at[mine, :, pl.ds(0, length)],
            send_sem=series_send.at[number], recv_sem=series_recv.at[number],
            device_id=where, device_id_type=MESH,
        ))
    for step in range(1, cuts):
        target = lax.rem(me + step, cuts)
        copies.append(pltpu.make_async_remote_copy(
            src_ref=bank_stage.at[target], dst_ref=bank_ref.at[me],
            send_sem=bank_send.at[step - 1], recv_sem=bank_recv.at[step - 1],
            device_id={"cuts": target}, device_id_type=MESH,
        ))
    for copy in copies:
        copy.start()
    own = [
        pltpu.make_async_copy(series_stage, series_ref.at[mine, :, pl.ds(0, length)], keep_sem.at[0]),
        pltpu.make_async_copy(bank_stage.at[me], bank_ref.at[me], keep_sem.at[1]),
    ]
    for copy in own:
        copy.start()
    for copy in own:
        copy.wait()
    for copy in copies:
        copy.wait()


def exchange(spans, strain, filters, weights, cuts, dets):
    rows = weights.shape[0] // cuts // dets
    taps = filters.shape[1]
    length = strain.shape[-1]
    vmem = pl.BlockSpec(memory_space=pltpu.VMEM)
    return pl.pallas_call(
        functools.partial(exchange_kernel, cuts, dets),
        out_shape=(
            jax.ShapeDtypeStruct((cuts, rows, taps), jnp.float32),
            jax.ShapeDtypeStruct((cuts * dets, 1, padded_length(length - taps, taps)), jnp.float32),
        ),
        in_specs=[vmem] * 4,
        out_specs=(vmem, vmem),
        scratch_shapes=[
            pltpu.VMEM((cuts, rows, taps), jnp.float32),
            pltpu.VMEM((1, length), jnp.float32),
            pltpu.SemaphoreType.DMA((cuts - 1,)),
            pltpu.SemaphoreType.DMA((cuts - 1,)),
            pltpu.SemaphoreType.DMA((cuts * dets - 1,)),
            pltpu.SemaphoreType.DMA((cuts * dets - 1,)),
            pltpu.SemaphoreType.DMA((2,)),
        ],
        compiler_params=pltpu.CompilerParams(collective_id=0, has_side_effects=True),
    )(spans, strain, filters, weights)


def padded_length(window, taps):
    steps = window // WIDE + taps // WIDE - 1
    return ((steps + BATCH - 1) // BATCH * BATCH * 2 + 1) * LANES


def search_kernel(
    rates_ref, delays_ref, antenna_ref, bank_ref, series_ref, peak_ref,
    toeplitz, total, combined, turned, best,
):
    slices, rows, taps = bank_ref.shape
    dets = series_ref.shape[0] // slices
    window = peak_ref.shape[1]
    tiles = window // LANES
    pieces = taps // WIDE
    combined[...] = jnp.zeros(combined.shape, jnp.float32)
    lane = lax.broadcasted_iota(jnp.int32, (rows, LANES), 1)
    ahead = lax.broadcasted_iota(jnp.int32, (LANES, LANES), 1) >= lax.broadcasted_iota(
        jnp.int32, (LANES, LANES), 0
    )

    def one_slice(number, carry):
        rate = rates_ref[number]
        level = (rate > 1).astype(jnp.int32) + (rate > 3).astype(jnp.int32) + (rate > 7).astype(jnp.int32)
        blocks = lax.shift_right_logical(jnp.int32(window // WIDE), level)
        batches = (blocks + pieces - 1 + BATCH - 1) // BATCH
        taps_all = bank_ref[number].astype(jnp.bfloat16)
        stacked = jnp.concatenate(
            [taps_all[:, piece * WIDE : (piece + 1) * WIDE] for piece in range(pieces)], axis=0
        )
        for det in range(dets):
            for at in range(2 * (pieces - 1)):
                total[det, at] = jnp.zeros((rows, LANES), jnp.float32)

        def build(batch, c):
            for det in range(dets):
                before = None
                for near in range(2 * BATCH + 1):
                    at = 2 * BATCH * batch + near
                    piece = series_ref[number * dets + det, :, pl.ds(pl.multiple_of(at * LANES, LANES), LANES)]
                    rolled = pltpu.roll(jnp.broadcast_to(piece, (LANES, LANES)), 0, 1, stride=1, stride_axis=0)
                    if near:
                        toeplitz[det, at - 1] = jnp.where(ahead, rolled, before).astype(jnp.bfloat16)
                    before = rolled
            return c

        lax.fori_loop(0, batches, build, 0)

        def convolve(batch, c):
            for det in range(dets):
                sums = [None] * (BATCH + pieces - 1)
                for near in range(BATCH):
                    at = 2 * (BATCH * batch + near)
                    low, middle, high = toeplitz[det, at], toeplitz[det, at + 1], toeplitz[det, at + 2]
                    square = jnp.concatenate(
                        [jnp.concatenate([middle, high], axis=1), jnp.concatenate([low, middle], axis=1)], axis=0
                    )
                    result = jnp.dot(stacked, square, preferred_element_type=jnp.float32)
                    for piece in range(pieces):
                        term = result[piece * rows : (piece + 1) * rows]
                        old = sums[near + piece]
                        sums[near + piece] = term if old is None else old + term
                for far, value in enumerate(sums):
                    for half in range(2):
                        at = 2 * (BATCH * batch + far) + half
                        part = value[:, half * LANES : (half + 1) * LANES]
                        total[det, at] = part if far >= pieces - 1 else total[det, at] + part
            return c

        lax.fori_loop(0, batches, convolve, 0)

        skip = 2 * (pieces - 1)
        inner = lax.shift_right_logical(lane, level)
        for tile in range(tiles):
            source = lax.shift_right_logical(jnp.int32(tile), level)
            part = tile - lax.shift_left(source, level)
            index = inner + part * lax.shift_right_logical(jnp.int32(LANES), level)
            for det in range(dets):
                values = total[det, skip + source]
                combined[det, tile] += jnp.take_along_axis(values, index, axis=1)
        return carry

    lax.fori_loop(0, slices, one_slice, 0)

    groups = LANES // rows
    apart = tiles // groups
    for det in range(dets):
        for offset in range(apart + 1):
            block = jnp.concatenate(
                [combined[det, group * apart + offset] for group in range(groups)], axis=0
            )
            turned[det, offset * LANES : (offset + 1) * LANES] = block.T

    for first in range(0, apart * LANES, CHUNK):
        def direction(number, highest):
            summed = None
            for det in range(dets):
                start = delays_ref[det, number] + first
                term = antenna_ref[det, number] * turned[det, pl.ds(start, CHUNK), :]
                summed = term if summed is None else summed + term
            return jnp.maximum(highest, jnp.abs(summed))

        best[first : first + CHUNK] = lax.fori_loop(
            0, delays_ref.shape[1], direction, jnp.zeros((CHUNK, LANES), jnp.float32), unroll=4
        )
    for offset in range(apart):
        back = best[offset * LANES : (offset + 1) * LANES].T
        for group in range(groups):
            at = (group * apart + offset) * LANES
            peak_ref[:, at : at + LANES] = back[group * rows : (group + 1) * rows]


def search(rates, delays, antenna, bank, series, window):
    slices, rows, taps = bank.shape
    dets = series.shape[0] // slices
    tiles = window // LANES
    pieces = taps // WIDE
    groups = LANES // rows
    apart = tiles // groups
    chunks = series.shape[2] // LANES
    smem = pl.BlockSpec(memory_space=pltpu.SMEM)
    vmem = pl.BlockSpec(memory_space=pltpu.VMEM)
    return pl.pallas_call(
        search_kernel,
        out_shape=jax.ShapeDtypeStruct((rows, window), jnp.float32),
        in_specs=[smem, smem, smem, vmem, vmem],
        out_specs=vmem,
        scratch_shapes=[
            pltpu.VMEM((dets, chunks, LANES, LANES), jnp.bfloat16),
            pltpu.VMEM((dets, chunks + 2 * pieces, rows, LANES), jnp.float32),
            pltpu.VMEM((dets, tiles + apart, rows, LANES), jnp.float32),
            pltpu.VMEM((dets, (apart + 1) * LANES, LANES), jnp.float32),
            pltpu.VMEM((apart * LANES, LANES), jnp.float32),
        ],
    )(rates, delays.T, antenna.T, bank, series)


def shards(strain, filters, recon_weights, row_spans, slice_rates, delays, antenna):
    cuts = lax.axis_size("cuts")
    dets = lax.axis_size("det")
    bank, series = exchange(
        row_spans.reshape(1, -1), strain.reshape(1, -1), filters[0], recon_weights[0], cuts, dets
    )
    window = strain.shape[-1] - filters.shape[-1]
    return search(slice_rates, delays, antenna, bank, series, window)


def solution(mesh):
    placed = (
        P("cuts", "det", None),
        P(("bank", "cuts"), None, None),
        P(("bank", "cuts"), None, None),
        P("bank"),
        P(),
        P(),
        P(),
    )
    return jax.shard_map(
        shards,
        mesh=mesh,
        in_specs=placed,
        out_specs=P(("bank", "cuts", "det"), None),
        check_vma=False,
    )
```

```python
import functools

import jax
import jax.numpy as jnp
from jax import lax
from jax.experimental import pallas as pl
from jax.experimental.pallas import tpu as pltpu
from jax.sharding import PartitionSpec as P

MESH = pl.DeviceIdType.MESH
LANES = 128
WIDE = 256
BATCH = 2
LEVELS = 4
CHUNK = 64


def exchange_kernel(
    cuts, dets, spans_ref, strain_ref, weights_ref, filters_hbm, bank_ref, series_ref,
    filters, bank_stage, series_stage, bank_send, bank_recv, cross_send, cross_recv, side_send, side_recv,
    local_sem,
):
    me = lax.axis_index("cuts")
    core = lax.axis_index("det")
    fetch = pltpu.make_async_copy(filters_hbm, filters, local_sem.at[0])
    fetch.start()
    barrier = pltpu.get_barrier_semaphore()
    for step in range(1, cuts):
        pl.semaphore_signal(
            barrier, inc=1, device_id={"cuts": lax.rem(me + step, cuts)}, device_id_type=MESH
        )
    for turn in range(1, dets):
        pl.semaphore_signal(
            barrier, inc=1, device_id={"det": lax.rem(core + turn, dets)}, device_id_type=MESH
        )

    series_stage[...] = strain_ref[...].astype(jnp.float32)
    rows = weights_ref.shape[0]
    share = rows // cuts // dets
    live = (me < spans_ref[...]).astype(jnp.float32)
    across = lax.broadcasted_iota(jnp.int32, (rows, rows), 1)
    down = lax.broadcasted_iota(jnp.int32, (rows, rows), 0)
    keep = jnp.sum(jnp.where(across == down, live, 0.0), axis=1, keepdims=True)
    kept = (weights_ref[...].astype(jnp.float32) * keep).astype(jnp.bfloat16)
    parts = []
    for cut in range(cuts):
        low = kept[(cut * dets) * share : (cut * dets + 1) * share]
        for det in range(1, dets):
            other = kept[(cut * dets + det) * share : (cut * dets + det + 1) * share]
            low = jnp.where(core == det, other, low)
        parts.append(low)
    stacked = jnp.concatenate(parts, axis=0)

    pl.semaphore_wait(barrier, cuts - 1 + dets - 1)
    mine = me * dets + core
    cross = []
    for step in range(1, cuts):
        cross.append(pltpu.make_async_remote_copy(
            src_ref=series_stage, dst_ref=series_ref.at[mine],
            send_sem=cross_send.at[step - 1], recv_sem=cross_recv.at[step - 1],
            device_id={"cuts": lax.rem(me + step, cuts)}, device_id_type=MESH,
        ))
    for copy in cross:
        copy.start()
    side = []
    for step in range(cuts):
        origin = lax.rem(me - step + cuts, cuts) * dets + core
        for turn in range(1, dets):
            number = step * (dets - 1) + turn - 1
            side.append(pltpu.make_async_remote_copy(
                src_ref=series_ref.at[origin] if step else series_stage, dst_ref=series_ref.at[origin],
                send_sem=side_send.at[number], recv_sem=side_recv.at[number],
                device_id={"det": lax.rem(core + turn, dets)}, device_id_type=MESH,
            ))
    for copy in side[: dets - 1]:
        copy.start()
    own = [
        pltpu.make_async_copy(series_stage, series_ref.at[mine], local_sem.at[1]),
        pltpu.make_async_copy(bank_stage.at[me], bank_ref.at[me], local_sem.at[2]),
    ]
    own[0].start()

    fetch.wait()
    taps = filters.shape[1]
    for first in range(0, taps, WIDE):
        block = jnp.dot(stacked, filters[:, first : first + WIDE], preferred_element_type=jnp.float32)
        for cut in range(cuts):
            bank_stage[cut, :, first : first + WIDE] = block[cut * share : (cut + 1) * share]
    banks = []
    for step in range(1, cuts):
        target = lax.rem(me + step, cuts)
        banks.append(pltpu.make_async_remote_copy(
            src_ref=bank_stage.at[target], dst_ref=bank_ref.at[me],
            send_sem=bank_send.at[step - 1], recv_sem=bank_recv.at[step - 1],
            device_id={"cuts": target}, device_id_type=MESH,
        ))
    for copy in banks:
        copy.start()
    own[1].start()
    for step in range(1, cuts):
        cross[step - 1].wait_recv()
        for turn in range(1, dets):
            side[step * (dets - 1) + turn - 1].start()
    for copy in own:
        copy.wait()
    for copy in cross:
        copy.wait_send()
    for copy in side:
        copy.wait()
    for copy in banks:
        copy.wait()


def exchange(spans, strain, filters, weights, cuts, dets):
    rows = weights.shape[0] // cuts // dets
    taps = filters.shape[1]
    length = strain.shape[-1]
    vmem = pl.BlockSpec(memory_space=pltpu.VMEM)
    hbm = pl.BlockSpec(memory_space=pltpu.HBM)
    dma = pltpu.SemaphoreType.DMA
    return pl.pallas_call(
        functools.partial(exchange_kernel, cuts, dets),
        out_shape=(
            jax.ShapeDtypeStruct((cuts, rows, taps), jnp.float32),
            jax.ShapeDtypeStruct((cuts * dets, 1, length), jnp.float32),
        ),
        in_specs=[vmem, vmem, vmem, hbm],
        out_specs=(hbm, hbm),
        scratch_shapes=[
            pltpu.VMEM(filters.shape, filters.dtype),
            pltpu.VMEM((cuts, rows, taps), jnp.float32),
            pltpu.VMEM((1, length), jnp.float32),
            dma((cuts - 1,)),
            dma((cuts - 1,)),
            dma((cuts - 1,)),
            dma((cuts - 1,)),
            dma((cuts * (dets - 1),)),
            dma((cuts * (dets - 1),)),
            dma((3,)),
        ],
        compiler_params=pltpu.CompilerParams(collective_id=0, has_side_effects=True),
    )(spans, strain, weights, filters)


def search_kernel(
    rates_ref, delays_ref, antenna_ref, bank_ref, series_ref, peak_ref,
    even, odd, total, combined, turned, best,
):
    slices, rows, taps = bank_ref.shape
    dets = series_ref.shape[0] // slices
    window = peak_ref.shape[1]
    tiles = window // LANES
    pieces = taps // WIDE
    chunks = series_ref.shape[2] // LANES
    combined[...] = jnp.zeros(combined.shape, jnp.float32)
    lane = lax.broadcasted_iota(jnp.int32, (rows, LANES), 1)
    ahead = lax.broadcasted_iota(jnp.int32, (LANES, LANES), 1) >= lax.broadcasted_iota(
        jnp.int32, (LANES, LANES), 0
    )

    def one_slice(number, carry):
        rate = rates_ref[number]
        level = (rate > 1).astype(jnp.int32) + (rate > 3).astype(jnp.int32) + (rate > 7).astype(jnp.int32)
        blocks = lax.shift_right_logical(jnp.int32(window // WIDE), level)
        batches = (blocks + pieces - 1 + 2 * BATCH - 1) // (2 * BATCH)
        taps_all = bank_ref[number].astype(jnp.bfloat16)
        stacked = jnp.concatenate(
            [taps_all[:, piece * WIDE : (piece + 1) * WIDE] for piece in range(pieces)], axis=0
        )
        for det in range(dets):
            for at in range(2 * (pieces - 1)):
                total[det, at] = jnp.zeros((rows, LANES), jnp.float32)

        def build(keep, first):
            for det in range(dets):
                before = None
                for near in range(2 * BATCH + 2):
                    at = pl.multiple_of(jnp.minimum(first + near, chunks - 1) * LANES, LANES)
                    piece = series_ref[number * dets + det, :, pl.ds(at, LANES)]
                    rolled = pltpu.roll(jnp.broadcast_to(piece, (LANES, LANES)), 0, 1, stride=1, stride_axis=0)
                    if near:
                        keep[det, near - 1] = jnp.where(ahead, rolled, before).astype(jnp.bfloat16)
                    before = rolled

        def multiply(keep, det, sums, start):
            for near in range(BATCH):
                low, middle, high = keep[det, 2 * near], keep[det, 2 * near + 1], keep[det, 2 * near + 2]
                square = jnp.concatenate(
                    [jnp.concatenate([middle, high], axis=1), jnp.concatenate([low, middle], axis=1)], axis=0
                )
                result = jnp.dot(stacked, square, preferred_element_type=jnp.float32)
                for piece in range(pieces):
                    term = result[piece * rows : (piece + 1) * rows]
                    old = sums[start + near + piece]
                    sums[start + near + piece] = term if old is None else old + term

        build(even, 0)

        def convolve(batch, c):
            base = 2 * BATCH * batch
            sums = [[None] * (2 * BATCH + pieces - 1) for det in range(dets)]
            build(odd, 2 * base + 2 * BATCH)
            for det in range(dets):
                multiply(even, det, sums[det], 0)
            build(even, 2 * base + 4 * BATCH)
            for det in range(dets):
                multiply(odd, det, sums[det], BATCH)
                for far, value in enumerate(sums[det]):
                    for half in range(2):
                        at = 2 * (base + far) + half
                        part = value[:, half * LANES : (half + 1) * LANES]
                        total[det, at] = part if far >= pieces - 1 else total[det, at] + part
            return c

        lax.fori_loop(0, batches, convolve, 0)

        skip = 2 * (pieces - 1)
        for known in range(LEVELS):
            @pl.when(level == known)
            def _(known=known):
                for tile in range(tiles):
                    index = lax.shift_right_logical(lane, known) + (tile % 2**known) * (LANES >> known)
                    for det in range(dets):
                        values = total[det, skip + (tile >> known)]
                        if known:
                            values = jnp.take_along_axis(values, index, axis=1)
                        combined[det, tile] += values
        return carry

    lax.fori_loop(0, slices, one_slice, 0)

    groups = LANES // rows
    apart = tiles // groups
    for det in range(dets):
        for offset in range(apart + 1):
            block = jnp.concatenate(
                [combined[det, group * apart + offset] for group in range(groups)], axis=0
            )
            turned[det, offset * LANES : (offset + 1) * LANES] = block.T

    for first in range(0, apart * LANES, CHUNK):
        def direction(number, highest):
            summed = None
            for det in range(dets):
                start = delays_ref[det, number] + first
                term = antenna_ref[det, number] * turned[det, pl.ds(start, CHUNK), :]
                summed = term if summed is None else summed + term
            return jnp.maximum(highest, jnp.abs(summed))

        best[first : first + CHUNK] = lax.fori_loop(
            0, delays_ref.shape[1], direction, jnp.zeros((CHUNK, LANES), jnp.float32), unroll=16
        )
    for offset in range(apart):
        back = best[offset * LANES : (offset + 1) * LANES].T
        for group in range(groups):
            at = (group * apart + offset) * LANES
            peak_ref[:, at : at + LANES] = back[group * rows : (group + 1) * rows]


def search(rates, delays, antenna, bank, series, window):
    slices, rows, taps = bank.shape
    dets = series.shape[0] // slices
    tiles = window // LANES
    pieces = taps // WIDE
    groups = LANES // rows
    apart = tiles // groups
    chunks = series.shape[2] // LANES
    smem = pl.BlockSpec(memory_space=pltpu.SMEM)
    vmem = pl.BlockSpec(memory_space=pltpu.VMEM)
    return pl.pallas_call(
        search_kernel,
        out_shape=jax.ShapeDtypeStruct((rows, window), jnp.float32),
        in_specs=[smem, smem, smem, vmem, vmem],
        out_specs=vmem,
        scratch_shapes=[
            pltpu.VMEM((dets, 2 * BATCH + 1, LANES, LANES), jnp.bfloat16),
            pltpu.VMEM((dets, 2 * BATCH + 1, LANES, LANES), jnp.bfloat16),
            pltpu.VMEM((dets, chunks + 4 * BATCH + 2 * pieces, rows, LANES), jnp.float32),
            pltpu.VMEM((dets, tiles + apart, rows, LANES), jnp.float32),
            pltpu.VMEM((dets, (apart + 1) * LANES, LANES), jnp.float32),
            pltpu.VMEM((apart * LANES, LANES), jnp.float32),
        ],
    )(rates, delays.T, antenna.T, bank, series)


def shards(strain, filters, recon_weights, row_spans, slice_rates, delays, antenna):
    cuts = lax.axis_size("cuts")
    dets = lax.axis_size("det")
    bank, series = exchange(
        row_spans.reshape(1, -1), strain.reshape(1, -1), filters[0], recon_weights[0], cuts, dets
    )
    window = strain.shape[-1] - filters.shape[-1]
    return search(slice_rates, delays, antenna, bank, series, window)


def solution(mesh):
    placed = (
        P("cuts", "det", None),
        P(("bank", "cuts"), None, None),
        P(("bank", "cuts"), None, None),
        P("bank"),
        P(),
        P(),
        P(),
    )
    return jax.shard_map(
        shards,
        mesh=mesh,
        in_specs=placed,
        out_specs=P(("bank", "cuts", "det"), None),
        check_vma=False,
    )
```

```python
import functools

import jax
import jax.numpy as jnp
from jax import lax
from jax.experimental import pallas as pl
from jax.experimental.pallas import tpu as pltpu
from jax.sharding import PartitionSpec as P

MESH = pl.DeviceIdType.MESH
LANES = 128
WIDE = 256
BATCH = 2
LEVELS = 4
CHUNK = 64


def exchange_kernel(
    cuts, dets, spans_ref, strain_ref, weights_ref, filters_hbm, bank_ref, series_ref,
    filters, bank_stage, series_stage, bank_send, bank_recv, cross_send, cross_recv, side_send, side_recv,
    local_sem,
):
    me = lax.axis_index("cuts")
    core = lax.axis_index("det")
    fetch = pltpu.make_async_copy(filters_hbm, filters, local_sem.at[0])
    fetch.start()
    barrier = pltpu.get_barrier_semaphore()
    for step in range(1, cuts):
        pl.semaphore_signal(
            barrier, inc=1, device_id={"cuts": lax.rem(me + step, cuts)}, device_id_type=MESH
        )
    for turn in range(1, dets):
        pl.semaphore_signal(
            barrier, inc=1, device_id={"det": lax.rem(core + turn, dets)}, device_id_type=MESH
        )

    series_stage[...] = strain_ref[...].astype(jnp.float32)
    rows = weights_ref.shape[0]
    share = rows // cuts // dets
    live = (me < spans_ref[...]).astype(jnp.float32)
    across = lax.broadcasted_iota(jnp.int32, (rows, rows), 1)
    down = lax.broadcasted_iota(jnp.int32, (rows, rows), 0)
    keep = jnp.sum(jnp.where(across == down, live, 0.0), axis=1, keepdims=True)
    kept = (weights_ref[...].astype(jnp.float32) * keep).astype(jnp.bfloat16)
    parts = []
    for cut in range(cuts):
        low = kept[(cut * dets) * share : (cut * dets + 1) * share]
        for det in range(1, dets):
            other = kept[(cut * dets + det) * share : (cut * dets + det + 1) * share]
            low = jnp.where(core == det, other, low)
        parts.append(low)
    stacked = jnp.concatenate(parts, axis=0)

    pl.semaphore_wait(barrier, cuts - 1 + dets - 1)
    mine = me * dets + core
    cross = []
    for step in range(1, cuts):
        cross.append(pltpu.make_async_remote_copy(
            src_ref=series_stage, dst_ref=series_ref.at[mine],
            send_sem=cross_send.at[step - 1], recv_sem=cross_recv.at[step - 1],
            device_id={"cuts": lax.rem(me + step, cuts)}, device_id_type=MESH,
        ))
    for copy in cross:
        copy.start()
    side = []
    for step in range(cuts):
        origin = lax.rem(me - step + cuts, cuts) * dets + core
        for turn in range(1, dets):
            number = step * (dets - 1) + turn - 1
            side.append(pltpu.make_async_remote_copy(
                src_ref=series_ref.at[origin] if step else series_stage, dst_ref=series_ref.at[origin],
                send_sem=side_send.at[number], recv_sem=side_recv.at[number],
                device_id={"det": lax.rem(core + turn, dets)}, device_id_type=MESH,
            ))
    for copy in side[: dets - 1]:
        copy.start()
    own = [
        pltpu.make_async_copy(series_stage, series_ref.at[mine], local_sem.at[1]),
        pltpu.make_async_copy(bank_stage.at[me], bank_ref.at[me], local_sem.at[2]),
    ]
    own[0].start()

    fetch.wait()
    taps = filters.shape[1]
    for first in range(0, taps, WIDE):
        block = jnp.dot(stacked, filters[:, first : first + WIDE], preferred_element_type=jnp.float32)
        for cut in range(cuts):
            bank_stage[cut, :, first : first + WIDE] = block[cut * share : (cut + 1) * share]
    banks = []
    for step in range(1, cuts):
        target = lax.rem(me + step, cuts)
        banks.append(pltpu.make_async_remote_copy(
            src_ref=bank_stage.at[target], dst_ref=bank_ref.at[me],
            send_sem=bank_send.at[step - 1], recv_sem=bank_recv.at[step - 1],
            device_id={"cuts": target}, device_id_type=MESH,
        ))
    for copy in banks:
        copy.start()
    own[1].start()
    for step in range(1, cuts):
        cross[step - 1].wait_recv()
        for turn in range(1, dets):
            side[step * (dets - 1) + turn - 1].start()
    for copy in own:
        copy.wait()
    for copy in cross:
        copy.wait_send()
    for copy in side:
        copy.wait()
    for copy in banks:
        copy.wait()


def exchange(spans, strain, filters, weights, cuts, dets):
    rows = weights.shape[0] // cuts // dets
    taps = filters.shape[1]
    length = strain.shape[-1]
    vmem = pl.BlockSpec(memory_space=pltpu.VMEM)
    hbm = pl.BlockSpec(memory_space=pltpu.HBM)
    dma = pltpu.SemaphoreType.DMA
    return pl.pallas_call(
        functools.partial(exchange_kernel, cuts, dets),
        out_shape=(
            jax.ShapeDtypeStruct((cuts, rows, taps), jnp.float32),
            jax.ShapeDtypeStruct((cuts * dets, 1, length), jnp.float32),
        ),
        in_specs=[vmem, vmem, vmem, hbm],
        out_specs=(hbm, hbm),
        scratch_shapes=[
            pltpu.VMEM(filters.shape, filters.dtype),
            pltpu.VMEM((cuts, rows, taps), jnp.float32),
            pltpu.VMEM((1, length), jnp.float32),
            dma((cuts - 1,)),
            dma((cuts - 1,)),
            dma((cuts - 1,)),
            dma((cuts - 1,)),
            dma((cuts * (dets - 1),)),
            dma((cuts * (dets - 1),)),
            dma((3,)),
        ],
        compiler_params=pltpu.CompilerParams(collective_id=0, has_side_effects=True),
    )(spans, strain, weights, filters)


def search_kernel(
    rates_ref, delays_ref, antenna_ref, bank_ref, series_ref, peak_ref,
    even, odd, last, total, combined, turned, best,
):
    slices, rows, taps = bank_ref.shape
    dets = series_ref.shape[0] // slices
    window = peak_ref.shape[1]
    tiles = window // LANES
    pieces = taps // WIDE
    chunks = series_ref.shape[2] // LANES
    combined[...] = jnp.zeros(combined.shape, jnp.float32)
    lane = lax.broadcasted_iota(jnp.int32, (rows, LANES), 1)
    ahead = lax.broadcasted_iota(jnp.int32, (LANES, LANES), 1) >= lax.broadcasted_iota(
        jnp.int32, (LANES, LANES), 0
    )

    def one_slice(number, carry):
        rate = rates_ref[number]
        level = (rate > 1).astype(jnp.int32) + (rate > 3).astype(jnp.int32) + (rate > 7).astype(jnp.int32)
        blocks = lax.shift_right_logical(jnp.int32(window // WIDE), level)
        batches = (blocks + pieces - 1 + 2 * BATCH - 1) // (2 * BATCH)
        taps_all = bank_ref[number].astype(jnp.bfloat16)
        stacked = jnp.concatenate(
            [taps_all[:, piece * WIDE : (piece + 1) * WIDE] for piece in range(pieces)], axis=0
        )
        for det in range(dets):
            for at in range(2 * (pieces - 1)):
                total[det, at] = jnp.zeros((rows, LANES), jnp.float32)

        def roll_of(det, at):
            at = pl.multiple_of(jnp.minimum(at, chunks - 1) * LANES, LANES)
            piece = series_ref[number * dets + det, :, pl.ds(at, LANES)]
            return pltpu.roll(jnp.broadcast_to(piece, (LANES, LANES)), 0, 1, stride=1, stride_axis=0)

        def build(keep, first, previous=None):
            for det in range(dets):
                if previous is None:
                    before = roll_of(det, first)
                    now = roll_of(det, first + 1)
                    keep[det, 0] = jnp.where(ahead, now, before).astype(jnp.bfloat16)
                    before = now
                else:
                    keep[det, 0] = previous[det, 2 * BATCH]
                    before = last[det].astype(jnp.float32)
                for near in range(1, 2 * BATCH + 1):
                    now = roll_of(det, first + near + 1)
                    keep[det, near] = jnp.where(ahead, now, before).astype(jnp.bfloat16)
                    before = now
                last[det] = before.astype(jnp.bfloat16)

        def multiply(keep, det, sums, start):
            for near in range(BATCH):
                low, middle, high = keep[det, 2 * near], keep[det, 2 * near + 1], keep[det, 2 * near + 2]
                square = jnp.concatenate(
                    [jnp.concatenate([middle, high], axis=1), jnp.concatenate([low, middle], axis=1)], axis=0
                )
                result = jnp.dot(stacked, square, preferred_element_type=jnp.float32)
                for piece in range(pieces):
                    term = result[piece * rows : (piece + 1) * rows]
                    old = sums[start + near + piece]
                    sums[start + near + piece] = term if old is None else old + term

        build(even, 0)

        def convolve(batch, c):
            base = 2 * BATCH * batch
            sums = [[None] * (2 * BATCH + pieces - 1) for det in range(dets)]
            build(odd, 2 * base + 2 * BATCH, even)
            for det in range(dets):
                multiply(even, det, sums[det], 0)
            build(even, 2 * base + 4 * BATCH, odd)
            for det in range(dets):
                multiply(odd, det, sums[det], BATCH)
                for far, value in enumerate(sums[det]):
                    for half in range(2):
                        at = 2 * (base + far) + half
                        part = value[:, half * LANES : (half + 1) * LANES]
                        total[det, at] = part if far >= pieces - 1 else total[det, at] + part
            return c

        lax.fori_loop(0, batches, convolve, 0)

        skip = 2 * (pieces - 1)
        for known in range(LEVELS):
            @pl.when(level == known)
            def _(known=known):
                for tile in range(tiles):
                    index = lax.shift_right_logical(lane, known) + (tile % 2**known) * (LANES >> known)
                    for det in range(dets):
                        values = total[det, skip + (tile >> known)]
                        if known:
                            values = jnp.take_along_axis(values, index, axis=1)
                        combined[det, tile] += values
        return carry

    lax.fori_loop(0, slices, one_slice, 0)

    groups = LANES // rows
    apart = tiles // groups
    for det in range(dets):
        for offset in range(apart + 1):
            block = jnp.concatenate(
                [combined[det, group * apart + offset] for group in range(groups)], axis=0
            )
            turned[det, offset * LANES : (offset + 1) * LANES] = block.T

    for first in range(0, apart * LANES, CHUNK):
        def direction(number, highest):
            summed = None
            for det in range(dets):
                start = delays_ref[det, number] + first
                term = antenna_ref[det, number] * turned[det, pl.ds(start, CHUNK), :]
                summed = term if summed is None else summed + term
            return jnp.maximum(highest, jnp.abs(summed))

        best[first : first + CHUNK] = lax.fori_loop(
            0, delays_ref.shape[1], direction, jnp.zeros((CHUNK, LANES), jnp.float32), unroll=16
        )
    for offset in range(apart):
        back = best[offset * LANES : (offset + 1) * LANES].T
        for group in range(groups):
            at = (group * apart + offset) * LANES
            peak_ref[:, at : at + LANES] = back[group * rows : (group + 1) * rows]


def search(rates, delays, antenna, bank, series, window):
    slices, rows, taps = bank.shape
    dets = series.shape[0] // slices
    tiles = window // LANES
    pieces = taps // WIDE
    groups = LANES // rows
    apart = tiles // groups
    chunks = series.shape[2] // LANES
    smem = pl.BlockSpec(memory_space=pltpu.SMEM)
    vmem = pl.BlockSpec(memory_space=pltpu.VMEM)
    return pl.pallas_call(
        search_kernel,
        out_shape=jax.ShapeDtypeStruct((rows, window), jnp.float32),
        in_specs=[smem, smem, smem, vmem, vmem],
        out_specs=vmem,
        scratch_shapes=[
            pltpu.VMEM((dets, 2 * BATCH + 1, LANES, LANES), jnp.bfloat16),
            pltpu.VMEM((dets, 2 * BATCH + 1, LANES, LANES), jnp.bfloat16),
            pltpu.VMEM((dets, LANES, LANES), jnp.bfloat16),
            pltpu.VMEM((dets, chunks + 4 * BATCH + 2 * pieces, rows, LANES), jnp.float32),
            pltpu.VMEM((dets, tiles + apart, rows, LANES), jnp.float32),
            pltpu.VMEM((dets, (apart + 1) * LANES, LANES), jnp.float32),
            pltpu.VMEM((apart * LANES, LANES), jnp.float32),
        ],
    )(rates, delays.T, antenna.T, bank, series)


def shards(strain, filters, recon_weights, row_spans, slice_rates, delays, antenna):
    cuts = lax.axis_size("cuts")
    dets = lax.axis_size("det")
    bank, series = exchange(
        row_spans.reshape(1, -1), strain.reshape(1, -1), filters[0], recon_weights[0], cuts, dets
    )
    window = strain.shape[-1] - filters.shape[-1]
    return search(slice_rates, delays, antenna, bank, series, window)


def solution(mesh):
    placed = (
        P("cuts", "det", None),
        P(("bank", "cuts"), None, None),
        P(("bank", "cuts"), None, None),
        P("bank"),
        P(),
        P(),
        P(),
    )
    return jax.shard_map(
        shards,
        mesh=mesh,
        in_specs=placed,
        out_specs=P(("bank", "cuts", "det"), None),
        check_vma=False,
    )
```

```python
import functools

import jax
import jax.numpy as jnp
from jax import lax
from jax.experimental import pallas as pl
from jax.experimental.pallas import tpu as pltpu
from jax.sharding import PartitionSpec as P

MESH = pl.DeviceIdType.MESH
LANES = 128
WIDE = 256
BATCH = 2
LEVELS = 4
CHUNK = 64


def exchange_kernel(
    cuts, dets, spans_ref, strain_ref, weights_ref, filters_hbm, bank_ref, series_ref,
    filters, bank_stage, series_stage, bank_send, bank_recv, cross_send, cross_recv, side_send, side_recv,
    local_sem,
):
    me = lax.axis_index("cuts")
    core = lax.axis_index("det")
    fetch = pltpu.make_async_copy(filters_hbm, filters, local_sem.at[0])
    fetch.start()
    barrier = pltpu.get_barrier_semaphore()
    for step in range(1, cuts):
        pl.semaphore_signal(
            barrier, inc=1, device_id={"cuts": lax.rem(me + step, cuts)}, device_id_type=MESH
        )
    for turn in range(1, dets):
        pl.semaphore_signal(
            barrier, inc=1, device_id={"det": lax.rem(core + turn, dets)}, device_id_type=MESH
        )

    series_stage[...] = strain_ref[...].astype(jnp.float32)
    rows = weights_ref.shape[0]
    share = rows // cuts // dets
    live = (me < spans_ref[...]).astype(jnp.float32)
    across = lax.broadcasted_iota(jnp.int32, (rows, rows), 1)
    down = lax.broadcasted_iota(jnp.int32, (rows, rows), 0)
    keep = jnp.sum(jnp.where(across == down, live, 0.0), axis=1, keepdims=True)
    kept = (weights_ref[...].astype(jnp.float32) * keep).astype(jnp.bfloat16)
    parts = []
    for cut in range(cuts):
        low = kept[(cut * dets) * share : (cut * dets + 1) * share]
        for det in range(1, dets):
            other = kept[(cut * dets + det) * share : (cut * dets + det + 1) * share]
            low = jnp.where(core == det, other, low)
        parts.append(low)
    stacked = jnp.concatenate(parts, axis=0)

    pl.semaphore_wait(barrier, cuts - 1 + dets - 1)
    mine = me * dets + core
    cross = []
    for step in range(1, cuts):
        cross.append(pltpu.make_async_remote_copy(
            src_ref=series_stage, dst_ref=series_ref.at[mine],
            send_sem=cross_send.at[step - 1], recv_sem=cross_recv.at[step - 1],
            device_id={"cuts": lax.rem(me + step, cuts)}, device_id_type=MESH,
        ))
    for copy in cross:
        copy.start()
    side = []
    for step in range(cuts):
        origin = lax.rem(me - step + cuts, cuts) * dets + core
        for turn in range(1, dets):
            number = step * (dets - 1) + turn - 1
            side.append(pltpu.make_async_remote_copy(
                src_ref=series_ref.at[origin] if step else series_stage, dst_ref=series_ref.at[origin],
                send_sem=side_send.at[number], recv_sem=side_recv.at[number],
                device_id={"det": lax.rem(core + turn, dets)}, device_id_type=MESH,
            ))
    for copy in side[: dets - 1]:
        copy.start()
    own = [
        pltpu.make_async_copy(series_stage, series_ref.at[mine], local_sem.at[1]),
        pltpu.make_async_copy(bank_stage.at[me], bank_ref.at[me], local_sem.at[2]),
    ]
    own[0].start()

    fetch.wait()
    taps = filters.shape[1]
    for first in range(0, taps, WIDE):
        block = jnp.dot(stacked, filters[:, first : first + WIDE], preferred_element_type=jnp.float32)
        for cut in range(cuts):
            bank_stage[cut, :, first : first + WIDE] = block[cut * share : (cut + 1) * share]
    banks = []
    for step in range(1, cuts):
        target = lax.rem(me + step, cuts)
        banks.append(pltpu.make_async_remote_copy(
            src_ref=bank_stage.at[target], dst_ref=bank_ref.at[me],
            send_sem=bank_send.at[step - 1], recv_sem=bank_recv.at[step - 1],
            device_id={"cuts": target}, device_id_type=MESH,
        ))
    for copy in banks:
        copy.start()
    own[1].start()
    for step in range(1, cuts):
        cross[step - 1].wait_recv()
        for turn in range(1, dets):
            side[step * (dets - 1) + turn - 1].start()
    for copy in own:
        copy.wait()
    for copy in cross:
        copy.wait_send()
    for copy in side:
        copy.wait()
    for copy in banks:
        copy.wait()


def exchange(spans, strain, filters, weights, cuts, dets):
    rows = weights.shape[0] // cuts // dets
    taps = filters.shape[1]
    length = strain.shape[-1]
    vmem = pl.BlockSpec(memory_space=pltpu.VMEM)
    hbm = pl.BlockSpec(memory_space=pltpu.HBM)
    dma = pltpu.SemaphoreType.DMA
    return pl.pallas_call(
        functools.partial(exchange_kernel, cuts, dets),
        out_shape=(
            jax.ShapeDtypeStruct((cuts, rows, taps), jnp.float32),
            jax.ShapeDtypeStruct((cuts * dets, 1, length), jnp.float32),
        ),
        in_specs=[vmem, vmem, vmem, hbm],
        out_specs=(hbm, hbm),
        scratch_shapes=[
            pltpu.VMEM(filters.shape, filters.dtype),
            pltpu.VMEM((cuts, rows, taps), jnp.float32),
            pltpu.VMEM((1, length), jnp.float32),
            dma((cuts - 1,)),
            dma((cuts - 1,)),
            dma((cuts - 1,)),
            dma((cuts - 1,)),
            dma((cuts * (dets - 1),)),
            dma((cuts * (dets - 1),)),
            dma((3,)),
        ],
        compiler_params=pltpu.CompilerParams(collective_id=0, has_side_effects=True),
    )(spans, strain, weights, filters)


def search_kernel(
    rates_ref, delays_ref, antenna_ref, bank_ref, series_ref, peak_ref,
    even, odd, last, total, combined, turned, best,
):
    slices, rows, taps = bank_ref.shape
    dets = series_ref.shape[0] // slices
    window = peak_ref.shape[1]
    tiles = window // LANES
    pieces = taps // WIDE
    chunks = series_ref.shape[2] // LANES
    combined[...] = jnp.zeros(combined.shape, jnp.float32)
    lane = lax.broadcasted_iota(jnp.int32, (rows, LANES), 1)
    ahead = lax.broadcasted_iota(jnp.int32, (LANES, LANES), 1) >= lax.broadcasted_iota(
        jnp.int32, (LANES, LANES), 0
    )

    def build(keep, number, first, previous=None):
        for det in range(dets):
            if previous is not None:
                keep[det, 0] = previous[det, 2 * BATCH]
                before = last[det].astype(jnp.float32)
            for near in range(1, 2 * BATCH + 1):
                at = pl.multiple_of(jnp.clip(first + near + 1, 0, chunks - 1) * LANES, LANES)
                piece = series_ref[number * dets + det, :, pl.ds(at, LANES)]
                now = pltpu.roll(jnp.broadcast_to(piece, (LANES, LANES)), 0, 1, stride=1, stride_axis=0)
                if previous is not None or near > 1:
                    keep[det, near] = jnp.where(ahead, now, before).astype(jnp.bfloat16)
                before = now
            last[det] = before.astype(jnp.bfloat16)

    for det in range(dets):
        for near in range(2):
            even[det, near] = jnp.zeros((LANES, LANES), jnp.bfloat16)
    build(even, 0, -2)

    def one_slice(number, carry):
        rate = rates_ref[number]
        level = (rate > 1).astype(jnp.int32) + (rate > 3).astype(jnp.int32) + (rate > 7).astype(jnp.int32)
        blocks = lax.shift_right_logical(jnp.int32(window // WIDE), level)
        batches = (blocks + pieces + 2 * BATCH - 1) // (2 * BATCH)
        taps_all = bank_ref[number].astype(jnp.bfloat16)
        stacked = jnp.concatenate(
            [taps_all[:, piece * WIDE : (piece + 1) * WIDE] for piece in range(pieces)], axis=0
        )
        for det in range(dets):
            for at in range(2 * pieces - 2):
                total[det, at] = jnp.zeros((rows, LANES), jnp.float32)

        def multiply(keep, det, sums, start):
            for near in range(BATCH):
                low, middle, high = keep[det, 2 * near], keep[det, 2 * near + 1], keep[det, 2 * near + 2]
                square = jnp.concatenate(
                    [jnp.concatenate([middle, high], axis=1), jnp.concatenate([low, middle], axis=1)], axis=0
                )
                result = jnp.dot(stacked, square, preferred_element_type=jnp.float32)
                for piece in range(pieces):
                    term = result[piece * rows : (piece + 1) * rows]
                    old = sums[start + near + piece]
                    sums[start + near + piece] = term if old is None else old + term

        def convolve(batch, c):
            base = 2 * BATCH * batch
            sums = [[None] * (2 * BATCH + pieces - 1) for det in range(dets)]
            build(odd, number, 2 * base + 2 * BATCH - 2, even)
            for det in range(dets):
                multiply(even, det, sums[det], 0)
            final = batch == batches - 1
            build(
                even,
                jnp.where(final, jnp.minimum(number + 1, slices - 1), number),
                jnp.where(final, -2, 2 * base + 4 * BATCH - 2),
                odd,
            )
            for det in range(dets):
                multiply(odd, det, sums[det], BATCH)
                for far, value in enumerate(sums[det]):
                    for half in range(2):
                        at = 2 * (base + far) + half
                        part = value[:, half * LANES : (half + 1) * LANES]
                        total[det, at] = part if far >= pieces - 1 else total[det, at] + part
            return c

        lax.fori_loop(0, batches, convolve, 0)

        skip = 2 * pieces
        for known in range(LEVELS):
            @pl.when(level == known)
            def _(known=known):
                for tile in range(tiles):
                    index = lax.shift_right_logical(lane, known) + (tile % 2**known) * (LANES >> known)
                    for det in range(dets):
                        values = total[det, skip + (tile >> known)]
                        if known:
                            values = jnp.take_along_axis(values, index, axis=1)
                        combined[det, tile] += values
        return carry

    lax.fori_loop(0, slices, one_slice, 0)

    groups = LANES // rows
    apart = tiles // groups
    for det in range(dets):
        for offset in range(apart + 1):
            block = jnp.concatenate(
                [combined[det, group * apart + offset] for group in range(groups)], axis=0
            )
            turned[det, offset * LANES : (offset + 1) * LANES] = block.T

    for first in range(0, apart * LANES, CHUNK):
        def direction(number, highest):
            summed = None
            for det in range(dets):
                start = delays_ref[det, number] + first
                term = antenna_ref[det, number] * turned[det, pl.ds(start, CHUNK), :]
                summed = term if summed is None else summed + term
            return jnp.maximum(highest, jnp.abs(summed))

        best[first : first + CHUNK] = lax.fori_loop(
            0, delays_ref.shape[1], direction, jnp.zeros((CHUNK, LANES), jnp.float32), unroll=16
        )
    for offset in range(apart):
        back = best[offset * LANES : (offset + 1) * LANES].T
        for group in range(groups):
            at = (group * apart + offset) * LANES
            peak_ref[:, at : at + LANES] = back[group * rows : (group + 1) * rows]


def search(rates, delays, antenna, bank, series, window):
    slices, rows, taps = bank.shape
    dets = series.shape[0] // slices
    tiles = window // LANES
    pieces = taps // WIDE
    groups = LANES // rows
    apart = tiles // groups
    chunks = series.shape[2] // LANES
    smem = pl.BlockSpec(memory_space=pltpu.SMEM)
    vmem = pl.BlockSpec(memory_space=pltpu.VMEM)
    return pl.pallas_call(
        search_kernel,
        out_shape=jax.ShapeDtypeStruct((rows, window), jnp.float32),
        in_specs=[smem, smem, smem, vmem, vmem],
        out_specs=vmem,
        scratch_shapes=[
            pltpu.VMEM((dets, 2 * BATCH + 1, LANES, LANES), jnp.bfloat16),
            pltpu.VMEM((dets, 2 * BATCH + 1, LANES, LANES), jnp.bfloat16),
            pltpu.VMEM((dets, LANES, LANES), jnp.bfloat16),
            pltpu.VMEM((dets, chunks + 4 * BATCH + 2 * pieces, rows, LANES), jnp.float32),
            pltpu.VMEM((dets, tiles + apart, rows, LANES), jnp.float32),
            pltpu.VMEM((dets, (apart + 1) * LANES, LANES), jnp.float32),
            pltpu.VMEM((apart * LANES, LANES), jnp.float32),
        ],
    )(rates, delays.T, antenna.T, bank, series)


def shards(strain, filters, recon_weights, row_spans, slice_rates, delays, antenna):
    cuts = lax.axis_size("cuts")
    dets = lax.axis_size("det")
    bank, series = exchange(
        row_spans.reshape(1, -1), strain.reshape(1, -1), filters[0], recon_weights[0], cuts, dets
    )
    window = strain.shape[-1] - filters.shape[-1]
    return search(slice_rates, delays, antenna, bank, series, window)


def solution(mesh):
    placed = (
        P("cuts", "det", None),
        P(("bank", "cuts"), None, None),
        P(("bank", "cuts"), None, None),
        P("bank"),
        P(),
        P(),
        P(),
    )
    return jax.shard_map(
        shards,
        mesh=mesh,
        in_specs=placed,
        out_specs=P(("bank", "cuts", "det"), None),
        check_vma=False,
    )
```

```python
import functools

import jax
import jax.numpy as jnp
from jax import lax
from jax.experimental import pallas as pl
from jax.experimental.pallas import tpu as pltpu
from jax.sharding import PartitionSpec as P

MESH = pl.DeviceIdType.MESH
LANES = 128
WIDE = 256
BATCH = 2
LEVELS = 4
CHUNK = 64


def exchange_kernel(
    cuts, dets, spans_hbm, strain_hbm, weights_hbm, filters_hbm, bank_ref, series_ref,
    spans_ref, strain_ref, weights_ref, filters, bank_stage, series_stage,
    bank_send, bank_recv, cross_send, cross_recv, side_send, side_recv,
    local_sem,
):
    me = lax.axis_index("cuts")
    core = lax.axis_index("det")
    barrier = pltpu.get_barrier_semaphore()
    for step in range(1, cuts):
        pl.semaphore_signal(
            barrier, inc=1, device_id={"cuts": lax.rem(me + step, cuts)}, device_id_type=MESH
        )
    for turn in range(1, dets):
        pl.semaphore_signal(
            barrier, inc=1, device_id={"det": lax.rem(core + turn, dets)}, device_id_type=MESH
        )

    fetches = [
        pltpu.make_async_copy(strain_hbm, strain_ref, local_sem.at[3]),
        pltpu.make_async_copy(spans_hbm, spans_ref, local_sem.at[4]),
        pltpu.make_async_copy(weights_hbm, weights_ref, local_sem.at[5]),
        pltpu.make_async_copy(filters_hbm, filters, local_sem.at[0]),
    ]
    for copy in fetches:
        copy.start()
    fetches[0].wait()
    series_stage[...] = strain_ref[...].astype(jnp.float32)
    pl.semaphore_wait(barrier, cuts - 1 + dets - 1)
    mine = me * dets + core
    cross = []
    for step in range(1, cuts):
        cross.append(pltpu.make_async_remote_copy(
            src_ref=series_stage, dst_ref=series_ref.at[mine],
            send_sem=cross_send.at[step - 1], recv_sem=cross_recv.at[step - 1],
            device_id={"cuts": lax.rem(me + step, cuts)}, device_id_type=MESH,
        ))
    for copy in cross:
        copy.start()
    side = []
    for step in range(cuts):
        origin = lax.rem(me - step + cuts, cuts) * dets + core
        for turn in range(1, dets):
            number = step * (dets - 1) + turn - 1
            side.append(pltpu.make_async_remote_copy(
                src_ref=series_ref.at[origin] if step else series_stage, dst_ref=series_ref.at[origin],
                send_sem=side_send.at[number], recv_sem=side_recv.at[number],
                device_id={"det": lax.rem(core + turn, dets)}, device_id_type=MESH,
            ))
    for copy in side[: dets - 1]:
        copy.start()
    own = [
        pltpu.make_async_copy(series_stage, series_ref.at[mine], local_sem.at[1]),
        pltpu.make_async_copy(bank_stage.at[me], bank_ref.at[me], local_sem.at[2]),
    ]
    own[0].start()

    fetches[1].wait()
    fetches[2].wait()
    rows = weights_ref.shape[0]
    share = rows // cuts // dets
    live = (me < spans_ref[...]).astype(jnp.float32)
    across = lax.broadcasted_iota(jnp.int32, (rows, rows), 1)
    down = lax.broadcasted_iota(jnp.int32, (rows, rows), 0)
    keep = jnp.sum(jnp.where(across == down, live, 0.0), axis=1, keepdims=True)
    kept = (weights_ref[...].astype(jnp.float32) * keep).astype(jnp.bfloat16)
    parts = []
    for cut in range(cuts):
        low = kept[(cut * dets) * share : (cut * dets + 1) * share]
        for det in range(1, dets):
            other = kept[(cut * dets + det) * share : (cut * dets + det + 1) * share]
            low = jnp.where(core == det, other, low)
        parts.append(low)
    stacked = jnp.concatenate(parts, axis=0)
    fetches[3].wait()
    taps = filters.shape[1]
    for first in range(0, taps, WIDE):
        block = jnp.dot(stacked, filters[:, first : first + WIDE], preferred_element_type=jnp.float32)
        for cut in range(cuts):
            bank_stage[cut, :, first : first + WIDE] = block[cut * share : (cut + 1) * share]
    banks = []
    for step in range(1, cuts):
        target = lax.rem(me + step, cuts)
        banks.append(pltpu.make_async_remote_copy(
            src_ref=bank_stage.at[target], dst_ref=bank_ref.at[me],
            send_sem=bank_send.at[step - 1], recv_sem=bank_recv.at[step - 1],
            device_id={"cuts": target}, device_id_type=MESH,
        ))
    for copy in banks:
        copy.start()
    own[1].start()
    for step in range(1, cuts):
        cross[step - 1].wait_recv()
        for turn in range(1, dets):
            side[step * (dets - 1) + turn - 1].start()
    for copy in own:
        copy.wait()
    for copy in cross:
        copy.wait_send()
    for copy in side:
        copy.wait()
    for copy in banks:
        copy.wait()


def exchange(spans, strain, filters, weights, cuts, dets):
    rows = weights.shape[0] // cuts // dets
    taps = filters.shape[1]
    length = strain.shape[-1]
    hbm = pl.BlockSpec(memory_space=pltpu.HBM)
    dma = pltpu.SemaphoreType.DMA
    return pl.pallas_call(
        functools.partial(exchange_kernel, cuts, dets),
        out_shape=(
            jax.ShapeDtypeStruct((cuts, rows, taps), jnp.float32),
            jax.ShapeDtypeStruct((cuts * dets, 1, length), jnp.float32),
        ),
        in_specs=[hbm] * 4,
        out_specs=(hbm, hbm),
        scratch_shapes=[
            pltpu.VMEM(spans.shape, spans.dtype),
            pltpu.VMEM(strain.shape, strain.dtype),
            pltpu.VMEM(weights.shape, weights.dtype),
            pltpu.VMEM(filters.shape, filters.dtype),
            pltpu.VMEM((cuts, rows, taps), jnp.float32),
            pltpu.VMEM((1, length), jnp.float32),
            dma((cuts - 1,)),
            dma((cuts - 1,)),
            dma((cuts - 1,)),
            dma((cuts - 1,)),
            dma((cuts * (dets - 1),)),
            dma((cuts * (dets - 1),)),
            dma((6,)),
        ],
        compiler_params=pltpu.CompilerParams(collective_id=0, has_side_effects=True),
    )(spans, strain, weights, filters)


def search_kernel(
    rates_ref, delays_ref, antenna_ref, bank_ref, series_ref, peak_ref,
    even, odd, last, total, combined, turned, best,
):
    slices, rows, taps = bank_ref.shape
    dets = series_ref.shape[0] // slices
    window = peak_ref.shape[1]
    tiles = window // LANES
    pieces = taps // WIDE
    chunks = series_ref.shape[2] // LANES
    combined[...] = jnp.zeros(combined.shape, jnp.float32)
    lane = lax.broadcasted_iota(jnp.int32, (rows, LANES), 1)
    ahead = lax.broadcasted_iota(jnp.int32, (LANES, LANES), 1) >= lax.broadcasted_iota(
        jnp.int32, (LANES, LANES), 0
    )

    def build(keep, number, first, previous=None):
        for det in range(dets):
            if previous is not None:
                keep[det, 0] = previous[det, 2 * BATCH]
                before = last[det].astype(jnp.float32)
            for near in range(1, 2 * BATCH + 1):
                at = pl.multiple_of(jnp.clip(first + near + 1, 0, chunks - 1) * LANES, LANES)
                piece = series_ref[number * dets + det, :, pl.ds(at, LANES)]
                now = pltpu.roll(jnp.broadcast_to(piece, (LANES, LANES)), 0, 1, stride=1, stride_axis=0)
                if previous is not None or near > 1:
                    keep[det, near] = jnp.where(ahead, now, before).astype(jnp.bfloat16)
                before = now
            last[det] = before.astype(jnp.bfloat16)

    for det in range(dets):
        for near in range(2):
            even[det, near] = jnp.zeros((LANES, LANES), jnp.bfloat16)
    build(even, 0, -2)

    def one_slice(number, carry):
        rate = rates_ref[number]
        level = (rate > 1).astype(jnp.int32) + (rate > 3).astype(jnp.int32) + (rate > 7).astype(jnp.int32)
        blocks = lax.shift_right_logical(jnp.int32(window // WIDE), level)
        batches = (blocks + pieces + 2 * BATCH - 1) // (2 * BATCH)
        taps_all = bank_ref[number].astype(jnp.bfloat16)
        stacked = jnp.concatenate(
            [taps_all[:, piece * WIDE : (piece + 1) * WIDE] for piece in range(pieces)], axis=0
        )
        for det in range(dets):
            for at in range(2 * pieces - 2):
                total[det, at] = jnp.zeros((rows, LANES), jnp.float32)

        def multiply(keep, det, sums, start):
            for near in range(BATCH):
                low, middle, high = keep[det, 2 * near], keep[det, 2 * near + 1], keep[det, 2 * near + 2]
                square = jnp.concatenate(
                    [jnp.concatenate([middle, high], axis=1), jnp.concatenate([low, middle], axis=1)], axis=0
                )
                result = jnp.dot(stacked, square, preferred_element_type=jnp.float32)
                for piece in range(pieces):
                    term = result[piece * rows : (piece + 1) * rows]
                    old = sums[start + near + piece]
                    sums[start + near + piece] = term if old is None else old + term

        def convolve(batch, c):
            base = 2 * BATCH * batch
            sums = [[None] * (2 * BATCH + pieces - 1) for det in range(dets)]
            build(odd, number, 2 * base + 2 * BATCH - 2, even)
            for det in range(dets):
                multiply(even, det, sums[det], 0)
            final = batch == batches - 1
            build(
                even,
                jnp.where(final, jnp.minimum(number + 1, slices - 1), number),
                jnp.where(final, -2, 2 * base + 4 * BATCH - 2),
                odd,
            )
            for det in range(dets):
                multiply(odd, det, sums[det], BATCH)
                for far, value in enumerate(sums[det]):
                    for half in range(2):
                        at = 2 * (base + far) + half
                        part = value[:, half * LANES : (half + 1) * LANES]
                        total[det, at] = part if far >= pieces - 1 else total[det, at] + part
            return c

        lax.fori_loop(0, batches, convolve, 0)

        skip = 2 * pieces
        for known in range(LEVELS):
            @pl.when(level == known)
            def _(known=known):
                for tile in range(tiles):
                    index = lax.shift_right_logical(lane, known) + (tile % 2**known) * (LANES >> known)
                    for det in range(dets):
                        values = total[det, skip + (tile >> known)]
                        if known:
                            values = jnp.take_along_axis(values, index, axis=1)
                        combined[det, tile] += values
        return carry

    lax.fori_loop(0, slices, one_slice, 0)

    groups = LANES // rows
    apart = tiles // groups
    for det in range(dets):
        for offset in range(apart + 1):
            block = jnp.concatenate(
                [combined[det, group * apart + offset] for group in range(groups)], axis=0
            )
            turned[det, offset * LANES : (offset + 1) * LANES] = block.T

    for first in range(0, apart * LANES, CHUNK):
        def direction(number, highest):
            summed = None
            for det in range(dets):
                start = delays_ref[det, number] + first
                term = antenna_ref[det, number] * turned[det, pl.ds(start, CHUNK), :]
                summed = term if summed is None else summed + term
            return jnp.maximum(highest, jnp.abs(summed))

        best[first : first + CHUNK] = lax.fori_loop(
            0, delays_ref.shape[1], direction, jnp.zeros((CHUNK, LANES), jnp.float32), unroll=16
        )
    for offset in range(apart):
        back = best[offset * LANES : (offset + 1) * LANES].T
        for group in range(groups):
            at = (group * apart + offset) * LANES
            peak_ref[:, at : at + LANES] = back[group * rows : (group + 1) * rows]


def search(rates, delays, antenna, bank, series, window):
    slices, rows, taps = bank.shape
    dets = series.shape[0] // slices
    tiles = window // LANES
    pieces = taps // WIDE
    groups = LANES // rows
    apart = tiles // groups
    chunks = series.shape[2] // LANES
    smem = pl.BlockSpec(memory_space=pltpu.SMEM)
    vmem = pl.BlockSpec(memory_space=pltpu.VMEM)
    return pl.pallas_call(
        search_kernel,
        out_shape=jax.ShapeDtypeStruct((rows, window), jnp.float32),
        in_specs=[smem, smem, smem, vmem, vmem],
        out_specs=vmem,
        scratch_shapes=[
            pltpu.VMEM((dets, 2 * BATCH + 1, LANES, LANES), jnp.bfloat16),
            pltpu.VMEM((dets, 2 * BATCH + 1, LANES, LANES), jnp.bfloat16),
            pltpu.VMEM((dets, LANES, LANES), jnp.bfloat16),
            pltpu.VMEM((dets, chunks + 4 * BATCH + 2 * pieces, rows, LANES), jnp.float32),
            pltpu.VMEM((dets, tiles + apart, rows, LANES), jnp.float32),
            pltpu.VMEM((dets, (apart + 1) * LANES, LANES), jnp.float32),
            pltpu.VMEM((apart * LANES, LANES), jnp.float32),
        ],
    )(rates, delays.T, antenna.T, bank, series)


def shards(strain, filters, recon_weights, row_spans, slice_rates, delays, antenna):
    cuts = lax.axis_size("cuts")
    dets = lax.axis_size("det")
    bank, series = exchange(
        row_spans.reshape(1, -1), strain.reshape(1, -1), filters[0], recon_weights[0], cuts, dets
    )
    window = strain.shape[-1] - filters.shape[-1]
    return search(slice_rates, delays, antenna, bank, series, window)


def solution(mesh):
    placed = (
        P("cuts", "det", None),
        P(("bank", "cuts"), None, None),
        P(("bank", "cuts"), None, None),
        P("bank"),
        P(),
        P(),
        P(),
    )
    return jax.shard_map(
        shards,
        mesh=mesh,
        in_specs=placed,
        out_specs=P(("bank", "cuts", "det"), None),
        check_vma=False,
    )
```

```python
import functools

import jax
import jax.numpy as jnp
from jax import lax
from jax.experimental import pallas as pl
from jax.experimental.pallas import tpu as pltpu
from jax.sharding import PartitionSpec as P

MESH = pl.DeviceIdType.MESH
LANES = 128
WIDE = 256
BATCH = 2
LEVELS = 4
CHUNK = 64


def exchange_kernel(
    cuts, dets, spans_hbm, strain_hbm, weights_hbm, filters_hbm, bank_ref, series_ref,
    spans_ref, strain_ref, weights_ref, filters, bank_stage, series_stage,
    bank_send, bank_recv, cross_send, cross_recv, side_send, side_recv,
    local_sem,
):
    me = lax.axis_index("cuts")
    core = lax.axis_index("det")
    barrier = pltpu.get_barrier_semaphore()
    for step in range(1, cuts):
        pl.semaphore_signal(
            barrier, inc=1, device_id={"cuts": lax.rem(me + step, cuts)}, device_id_type=MESH
        )
    for turn in range(1, dets):
        pl.semaphore_signal(
            barrier, inc=1, device_id={"det": lax.rem(core + turn, dets)}, device_id_type=MESH
        )

    fetches = [
        pltpu.make_async_copy(strain_hbm, strain_ref, local_sem.at[3]),
        pltpu.make_async_copy(spans_hbm, spans_ref, local_sem.at[4]),
        pltpu.make_async_copy(weights_hbm, weights_ref, local_sem.at[5]),
        pltpu.make_async_copy(filters_hbm, filters, local_sem.at[0]),
    ]
    for copy in fetches:
        copy.start()
    fetches[0].wait()
    series_stage[...] = strain_ref[...].astype(jnp.float32)
    pl.semaphore_wait(barrier, cuts - 1 + dets - 1)
    mine = me * dets + core
    cross = []
    for step in range(1, cuts):
        cross.append(pltpu.make_async_remote_copy(
            src_ref=series_stage, dst_ref=series_ref.at[mine],
            send_sem=cross_send.at[step - 1], recv_sem=cross_recv.at[step - 1],
            device_id={"cuts": lax.rem(me + step, cuts)}, device_id_type=MESH,
        ))
    for copy in cross:
        copy.start()
    side = []
    for step in range(cuts):
        origin = lax.rem(me - step + cuts, cuts) * dets + core
        for turn in range(1, dets):
            number = step * (dets - 1) + turn - 1
            side.append(pltpu.make_async_remote_copy(
                src_ref=series_ref.at[origin] if step else series_stage, dst_ref=series_ref.at[origin],
                send_sem=side_send.at[number], recv_sem=side_recv.at[number],
                device_id={"det": lax.rem(core + turn, dets)}, device_id_type=MESH,
            ))
    for copy in side[: dets - 1]:
        copy.start()
    own = [
        pltpu.make_async_copy(series_stage, series_ref.at[mine], local_sem.at[1]),
        pltpu.make_async_copy(bank_stage.at[me], bank_ref.at[me], local_sem.at[2]),
    ]
    own[0].start()

    fetches[1].wait()
    fetches[2].wait()
    rows = weights_ref.shape[0]
    share = rows // cuts // dets
    live = (me < spans_ref[...]).astype(jnp.float32)
    across = lax.broadcasted_iota(jnp.int32, (rows, rows), 1)
    down = lax.broadcasted_iota(jnp.int32, (rows, rows), 0)
    keep = jnp.sum(jnp.where(across == down, live, 0.0), axis=1, keepdims=True)
    kept = (weights_ref[...].astype(jnp.float32) * keep).astype(jnp.bfloat16)
    parts = []
    for cut in range(cuts):
        low = kept[(cut * dets) * share : (cut * dets + 1) * share]
        for det in range(1, dets):
            other = kept[(cut * dets + det) * share : (cut * dets + det + 1) * share]
            low = jnp.where(core == det, other, low)
        parts.append(low)
    stacked = jnp.concatenate(parts, axis=0)
    fetches[3].wait()
    taps = filters.shape[1]
    for first in range(0, taps, WIDE):
        block = jnp.dot(stacked, filters[:, first : first + WIDE], preferred_element_type=jnp.float32)
        for cut in range(cuts):
            bank_stage[cut, :, first : first + WIDE] = block[cut * share : (cut + 1) * share]
    banks = []
    for step in range(1, cuts):
        target = lax.rem(me + step, cuts)
        banks.append(pltpu.make_async_remote_copy(
            src_ref=bank_stage.at[target], dst_ref=bank_ref.at[me],
            send_sem=bank_send.at[step - 1], recv_sem=bank_recv.at[step - 1],
            device_id={"cuts": target}, device_id_type=MESH,
        ))
    for copy in banks:
        copy.start()
    own[1].start()
    for step in range(1, cuts):
        cross[step - 1].wait_recv()
        for turn in range(1, dets):
            side[step * (dets - 1) + turn - 1].start()
    for copy in own:
        copy.wait()
    for copy in cross:
        copy.wait_send()
    for copy in side:
        copy.wait()
    for copy in banks:
        copy.wait()


def exchange(spans, strain, filters, weights, cuts, dets):
    rows = weights.shape[0] // cuts // dets
    taps = filters.shape[1]
    length = strain.shape[-1]
    hbm = pl.BlockSpec(memory_space=pltpu.HBM)
    dma = pltpu.SemaphoreType.DMA
    return pl.pallas_call(
        functools.partial(exchange_kernel, cuts, dets),
        out_shape=(
            jax.ShapeDtypeStruct((cuts, rows, taps), jnp.float32),
            jax.ShapeDtypeStruct((cuts * dets, 1, length), jnp.float32),
        ),
        in_specs=[hbm] * 4,
        out_specs=(hbm, hbm),
        scratch_shapes=[
            pltpu.VMEM(spans.shape, spans.dtype),
            pltpu.VMEM(strain.shape, strain.dtype),
            pltpu.VMEM(weights.shape, weights.dtype),
            pltpu.VMEM(filters.shape, filters.dtype),
            pltpu.VMEM((cuts, rows, taps), jnp.float32),
            pltpu.VMEM((1, length), jnp.float32),
            dma((cuts - 1,)),
            dma((cuts - 1,)),
            dma((cuts - 1,)),
            dma((cuts - 1,)),
            dma((cuts * (dets - 1),)),
            dma((cuts * (dets - 1),)),
            dma((6,)),
        ],
        compiler_params=pltpu.CompilerParams(collective_id=0, has_side_effects=True),
    )(spans, strain, weights, filters)


def search_kernel(
    rates_ref, delays_ref, antenna_ref, bank_hbm, series_ref, peak_ref,
    bank_ref, bank_sem, even, odd, last, total, combined, turned, best,
):
    fetch = pltpu.make_async_copy(bank_hbm, bank_ref, bank_sem)
    fetch.start()
    slices, rows, taps = bank_ref.shape
    dets = series_ref.shape[0] // slices
    window = peak_ref.shape[1]
    tiles = window // LANES
    pieces = taps // WIDE
    chunks = series_ref.shape[2] // LANES
    combined[...] = jnp.zeros(combined.shape, jnp.float32)
    lane = lax.broadcasted_iota(jnp.int32, (rows, LANES), 1)
    ahead = lax.broadcasted_iota(jnp.int32, (LANES, LANES), 1) >= lax.broadcasted_iota(
        jnp.int32, (LANES, LANES), 0
    )

    def build(keep, number, first, previous=None):
        for det in range(dets):
            if previous is not None:
                keep[det, 0] = previous[det, 2 * BATCH]
                before = last[det].astype(jnp.float32)
            for near in range(1, 2 * BATCH + 1):
                at = pl.multiple_of(jnp.clip(first + near + 1, 0, chunks - 1) * LANES, LANES)
                piece = series_ref[number * dets + det, :, pl.ds(at, LANES)]
                now = pltpu.roll(jnp.broadcast_to(piece, (LANES, LANES)), 0, 1, stride=1, stride_axis=0)
                if previous is not None or near > 1:
                    keep[det, near] = jnp.where(ahead, now, before).astype(jnp.bfloat16)
                before = now
            last[det] = before.astype(jnp.bfloat16)

    for det in range(dets):
        for near in range(2):
            even[det, near] = jnp.zeros((LANES, LANES), jnp.bfloat16)
    build(even, 0, -2)
    fetch.wait()

    def one_slice(number, carry):
        rate = rates_ref[number]
        level = (rate > 1).astype(jnp.int32) + (rate > 3).astype(jnp.int32) + (rate > 7).astype(jnp.int32)
        blocks = lax.shift_right_logical(jnp.int32(window // WIDE), level)
        batches = (blocks + pieces + 2 * BATCH - 1) // (2 * BATCH)
        taps_all = bank_ref[number].astype(jnp.bfloat16)
        stacked = jnp.concatenate(
            [taps_all[:, piece * WIDE : (piece + 1) * WIDE] for piece in range(pieces)], axis=0
        )
        for det in range(dets):
            for at in range(2 * pieces - 2):
                total[det, at] = jnp.zeros((rows, LANES), jnp.float32)

        def multiply(keep, det, sums, start):
            for near in range(BATCH):
                low, middle, high = keep[det, 2 * near], keep[det, 2 * near + 1], keep[det, 2 * near + 2]
                square = jnp.concatenate(
                    [jnp.concatenate([middle, high], axis=1), jnp.concatenate([low, middle], axis=1)], axis=0
                )
                result = jnp.dot(stacked, square, preferred_element_type=jnp.float32)
                for piece in range(pieces):
                    term = result[piece * rows : (piece + 1) * rows]
                    old = sums[start + near + piece]
                    sums[start + near + piece] = term if old is None else old + term

        def convolve(batch, c):
            base = 2 * BATCH * batch
            sums = [[None] * (2 * BATCH + pieces - 1) for det in range(dets)]
            build(odd, number, 2 * base + 2 * BATCH - 2, even)
            for det in range(dets):
                multiply(even, det, sums[det], 0)
            final = batch == batches - 1
            build(
                even,
                jnp.where(final, jnp.minimum(number + 1, slices - 1), number),
                jnp.where(final, -2, 2 * base + 4 * BATCH - 2),
                odd,
            )
            for det in range(dets):
                multiply(odd, det, sums[det], BATCH)
                for far, value in enumerate(sums[det]):
                    for half in range(2):
                        at = 2 * (base + far) + half
                        part = value[:, half * LANES : (half + 1) * LANES]
                        total[det, at] = part if far >= pieces - 1 else total[det, at] + part
            return c

        lax.fori_loop(0, batches, convolve, 0)

        skip = 2 * pieces
        for known in range(LEVELS):
            @pl.when(level == known)
            def _(known=known):
                for tile in range(tiles):
                    index = lax.shift_right_logical(lane, known) + (tile % 2**known) * (LANES >> known)
                    for det in range(dets):
                        values = total[det, skip + (tile >> known)]
                        if known:
                            values = jnp.take_along_axis(values, index, axis=1)
                        combined[det, tile] += values
        return carry

    lax.fori_loop(0, slices, one_slice, 0)

    groups = LANES // rows
    apart = tiles // groups
    for det in range(dets):
        for offset in range(apart + 1):
            block = jnp.concatenate(
                [combined[det, group * apart + offset] for group in range(groups)], axis=0
            )
            turned[det, offset * LANES : (offset + 1) * LANES] = block.T

    for first in range(0, apart * LANES, CHUNK):
        def direction(number, highest):
            summed = None
            for det in range(dets):
                start = delays_ref[det, number] + first
                term = antenna_ref[det, number] * turned[det, pl.ds(start, CHUNK), :]
                summed = term if summed is None else summed + term
            return jnp.maximum(highest, jnp.abs(summed))

        best[first : first + CHUNK] = lax.fori_loop(
            0, delays_ref.shape[1], direction, jnp.zeros((CHUNK, LANES), jnp.float32), unroll=16
        )
    for offset in range(apart):
        back = best[offset * LANES : (offset + 1) * LANES].T
        for group in range(groups):
            at = (group * apart + offset) * LANES
            peak_ref[:, at : at + LANES] = back[group * rows : (group + 1) * rows]


def search(rates, delays, antenna, bank, series, window):
    slices, rows, taps = bank.shape
    dets = series.shape[0] // slices
    tiles = window // LANES
    pieces = taps // WIDE
    groups = LANES // rows
    apart = tiles // groups
    chunks = series.shape[2] // LANES
    smem = pl.BlockSpec(memory_space=pltpu.SMEM)
    vmem = pl.BlockSpec(memory_space=pltpu.VMEM)
    return pl.pallas_call(
        search_kernel,
        out_shape=jax.ShapeDtypeStruct((rows, window), jnp.float32),
        in_specs=[smem, smem, smem, pl.BlockSpec(memory_space=pltpu.HBM), vmem],
        out_specs=vmem,
        scratch_shapes=[
            pltpu.VMEM(bank.shape, bank.dtype),
            pltpu.SemaphoreType.DMA,
            pltpu.VMEM((dets, 2 * BATCH + 1, LANES, LANES), jnp.bfloat16),
            pltpu.VMEM((dets, 2 * BATCH + 1, LANES, LANES), jnp.bfloat16),
            pltpu.VMEM((dets, LANES, LANES), jnp.bfloat16),
            pltpu.VMEM((dets, chunks + 4 * BATCH + 2 * pieces, rows, LANES), jnp.float32),
            pltpu.VMEM((dets, tiles + apart, rows, LANES), jnp.float32),
            pltpu.VMEM((dets, (apart + 1) * LANES, LANES), jnp.float32),
            pltpu.VMEM((apart * LANES, LANES), jnp.float32),
        ],
    )(rates, delays.T, antenna.T, bank, series)


def shards(strain, filters, recon_weights, row_spans, slice_rates, delays, antenna):
    cuts = lax.axis_size("cuts")
    dets = lax.axis_size("det")
    bank, series = exchange(
        row_spans.reshape(1, -1), strain.reshape(1, -1), filters[0], recon_weights[0], cuts, dets
    )
    window = strain.shape[-1] - filters.shape[-1]
    return search(slice_rates, delays, antenna, bank, series, window)


def solution(mesh):
    placed = (
        P("cuts", "det", None),
        P(("bank", "cuts"), None, None),
        P(("bank", "cuts"), None, None),
        P("bank"),
        P(),
        P(),
        P(),
    )
    return jax.shard_map(
        shards,
        mesh=mesh,
        in_specs=placed,
        out_specs=P(("bank", "cuts", "det"), None),
        check_vma=False,
    )
```
